32 devices in a mesh: shard: 16 (over z, y, x), tensor: 2 (over core).
Axes of the slice: x: 2, y: 2, z: 4, core: 2. Of those that a mesh axis runs over, the one named last changes fastest.
Arguments:
- tokens: bfloat16 [256, 197, 384], P('shard'), may hold values from -6 to 6
- image_counts: int32 [16], P('shard'), may hold values from 8 to 16, as said below
- input_weight: bfloat16 [3, 384, 384], P(None, 'shard', 'tensor')
- query_value_bias: bfloat16 [2, 2, 192], P(None, 'tensor', 'shard'), may hold values from -3 to 3
- output_weight: bfloat16 [384, 384], P('tensor', 'shard'), may hold values from -1.75 to 1.75
- output_bias: bfloat16 [384], P('shard'), may hold values from -3 to 3
- first_gain: bfloat16 [384], P('shard'), may hold values from 0.5 to 1.5
- first_shift: bfloat16 [384], P('shard'), may hold values from -3 to 3
- second_gain: bfloat16 [384], P('shard'), may hold values from 0.5 to 1.5
- second_shift: bfloat16 [384], P('shard'), may hold values from -3 to 3
- expand_weight: bfloat16 [384, 1536], P('shard', 'tensor'), may hold values from -0.3125 to 0.3125
- expand_bias: bfloat16 [2, 768], P('tensor', 'shard'), may hold values from -3 to 3
- reduce_weight: bfloat16 [1536, 384], P('tensor', 'shard'), may hold values from -0.3125 to 0.3125
- reduce_bias: bfloat16 [384], P('shard'), may hold values from -3 to 3
- cotangent: bfloat16 [256, 197, 384], P('shard'), may hold values from -6 to 6
Outputs:
- mixed: bfloat16 [256, 197, 384], P('shard')
- token_grad: bfloat16 [256, 197, 384], P('shard')
- input_weight_grad: float32 [3, 384, 384], P(None, 'shard', 'tensor')
- query_value_bias_grad: float32 [2, 2, 192], P(None, 'tensor', 'shard')
- output_weight_grad: float32 [384, 384], P('tensor', 'shard')
- output_bias_grad: float32 [384], P('shard')
- first_gain_grad: float32 [384], P('shard')
- first_shift_grad: float32 [384], P('shard')
- second_gain_grad: float32 [384], P('shard')
- second_shift_grad: float32 [384], P('shard')
- expand_weight_grad: float32 [384, 1536], P('shard', 'tensor')
- expand_bias_grad: float32 [2, 768], P('tensor', 'shard')
- reduce_weight_grad: float32 [1536, 384], P('tensor', 'shard')
- reduce_bias_grad: float32 [384], P('shard')
The draws below stay inside these ranges and needn't reach their ends.
Inputs may be any that keep to these rules, and one draw needn't show every extreme that they name: `image_counts`: every index of shard holds at least half of its 16 slots (at least one) filled; some index fills all, some exactly the least.
All inputs are finite; a program needn't handle non-finite values.
Results may differ from the reference program's by a relative error of at most 0.029.
Values may be sent and summed in bfloat16 or wider, within the bound.
No kernel may reach another device: no remote copies, remote signals or barrier semaphores. Data moves between devices by JAX's collectives and lax.ppermute only.
A program may use at most 128 MiB of HBM per device.

```python
import jax
import jax.numpy as jnp
from jax import lax

D = 384
HEADS = 6
FF = 1536
SEQ = 197
IMG_CAP = 16
HEAD = 64
SLOTS = 256
N_SHARD = 16
N_TENSOR = 2


def draw_image_counts(key, part):
    least = max(1, IMG_CAP // 2)
    counts = jax.random.randint(key, (N_SHARD,), least, IMG_CAP + 1)
    order = jax.random.permutation(jax.random.fold_in(key, 1), N_SHARD)
    counts = counts.at[order[0]].set(IMG_CAP)
    counts = counts.at[order[1]].set(least)
    return counts.astype(jnp.int32)


def draw_input_weight(key, part):
    base = jax.random.normal(key, (3, D, D), jnp.float32) * D ** (-0.5)
    return base.astype(jnp.bfloat16)


def shard_levels(key, extent, shards, low, largest):
    factor_of = 1.0
    for position, parts in shards:
        heights = jax.random.uniform(jax.random.fold_in(jax.random.fold_in(key, 6), position), (parts,), jnp.float32, low / len(shards), largest / len(shards))
        factor_of = factor_of * jnp.repeat(jnp.exp(heights), extent[position] // parts).reshape((-1,) + (1,) * (len(extent) - 1 - position))
    return factor_of


def normal_values(own_key, extent, deviation, reach, cuts=(), held_as=jnp.bfloat16):
    entries = jax.random.normal(own_key, extent, jnp.float32) * deviation
    if len(cuts) > 0:
        entries = shard_levels(own_key, extent, cuts, -0.22, 0.18) * entries
    return jnp.clip(entries, min=-reach, max=reach).astype(held_as)


def setup_inputs(seed: int = 0) -> dict:
    seeds = jax.random.split(jax.random.key(seed), 16)
    return {
        "tokens": normal_values(seeds[0], (SLOTS, SEQ, D), 1.0, 6.0, ((0, 16),)),
        "image_counts": draw_image_counts(jax.random.fold_in(seeds[15], 71), 0),
        "input_weight": draw_input_weight(jax.random.fold_in(seeds[15], 71), 0),
        "query_value_bias": normal_values(seeds[3], (2, N_TENSOR, D // N_TENSOR), 0.5, 3.0, ((1, 2), (2, 16))),
        "output_weight": normal_values(seeds[4], (D, D), (D // 32) ** -0.5, 1.75, ((0, 2), (1, 16))),
        "output_bias": normal_values(seeds[5], (D,), 0.5, 3.0, ((0, 16),)),
        "first_gain": jnp.clip(1.0 + 0.1 * jax.random.normal(seeds[6], (D,), jnp.float32), 0.5, 1.5).astype(jnp.bfloat16),
        "first_shift": normal_values(seeds[7], (D,), 0.5, 3.0, ((0, 16),)),
        "second_gain": jnp.clip(1.0 + 0.1 * jax.random.normal(seeds[8], (D,), jnp.float32), 0.5, 1.5).astype(jnp.bfloat16),
        "second_shift": normal_values(seeds[9], (D,), 0.5, 3.0, ((0, 16),)),
        "expand_weight": normal_values(seeds[10], (D, FF), D ** -0.5, 0.3125, ((0, 16), (1, 2))),
        "expand_bias": normal_values(seeds[11], (N_TENSOR, FF // N_TENSOR), 0.5, 3.0, ((0, 2), (1, 16))),
        "reduce_weight": normal_values(seeds[12], (FF, D), (FF // 4) ** -0.5, 0.3125, ((0, 2), (1, 16))),
        "reduce_bias": normal_values(seeds[13], (D,), 0.5, 3.0, ((0, 16),)),
        "cotangent": normal_values(seeds[14], (SLOTS, SEQ, D), 1.0, 6.0, ((0, 16),)),
    }


@jax.custom_vjp
def low(v):
    return lax.optimization_barrier(v.astype(jnp.bfloat16)).astype(jnp.float32)

@jax.custom_vjp
def low_back(v):
    return v

def low_keep(v):
    return (low(v), None)

def low_pass(kept, grad):
    return (grad,)

def back_keep(v):
    return (v, None)

def back_low(kept, grad):
    return (low(grad),)
low.defvjp(low_keep, low_pass)
low_back.defvjp(back_keep, back_low)
EPSILON = 1e-06
HIGHEST = lax.Precision.HIGHEST

def layer_norm(hidden, gain, shift):
    center = hidden - lax.optimization_barrier(jnp.mean(hidden, -1, keepdims=True))
    spread = lax.optimization_barrier(jnp.mean(center * center, -1, keepdims=True))
    return center * lax.rsqrt(spread + EPSILON) * gain + shift

def project(inputs, weight):
    return jnp.einsum('csd,de->cse', inputs, weight, precision=HIGHEST)

def block_forward(params, hidden):
    input_weight, query_value_bias, output_weight, output_bias, first_gain, first_shift, second_gain, second_shift, expand_weight, expand_bias, reduce_weight, reduce_bias = params
    images, length, features = hidden.shape
    head_shape = (images, length, HEADS, HEAD)
    normed_one = low(layer_norm(hidden, first_gain, first_shift))
    queries = low_back(low((project(normed_one, input_weight[0]) + query_value_bias[0].reshape(features)) * 0.125))
    key_rows = low_back(low(project(normed_one, input_weight[1])))
    values = low_back(low(project(normed_one, input_weight[2]) + query_value_bias[1].reshape(features)))
    scores = low_back(jnp.einsum('cqhe,ckhe->chqk', queries.reshape(head_shape), key_rows.reshape(head_shape), precision=HIGHEST))
    weights_low = low(jax.nn.softmax(scores, axis=-1))
    attended = jnp.einsum('chqk,ckhe->cqhe', weights_low, values.reshape(head_shape), precision=HIGHEST)
    attended = low_back(low(attended.reshape(images, length, features)))
    middle = hidden + low_back(project(attended, output_weight)) + output_bias
    normed_two = low(layer_norm(middle, second_gain, second_shift))
    before = low_back(project(normed_two, expand_weight) + expand_bias.reshape(-1))
    activated = low_back(low(jax.nn.gelu(before, approximate=False)))
    return middle + low_back(project(activated, reduce_weight)) + reduce_bias

def reference(tokens, image_counts, input_weight, query_value_bias, output_weight, output_bias, first_gain, first_shift, second_gain, second_shift, expand_weight, expand_bias, reduce_weight, reduce_bias, cotangent):
    params = jax.tree.map(lambda array: array.astype(jnp.float32), (input_weight, query_value_bias, output_weight, output_bias, first_gain, first_shift, second_gain, second_shift, expand_weight, expand_bias, reduce_weight, reduce_bias))
    live = (jnp.arange(IMG_CAP, dtype=jnp.int32)[None, :] < image_counts[:, None]).astype(jnp.float32)
    live = live[:, :, None, None]
    grouped = tokens.astype(jnp.float32).reshape(N_SHARD, IMG_CAP, SEQ, D)
    checked = jax.checkpoint(block_forward)

    def forward(weights_all, inputs_all):
        return lax.map(lambda image_block: checked(weights_all, image_block), inputs_all)
    outputs, pullback = jax.vjp(forward, params, grouped)
    grad_top = cotangent.astype(jnp.float32).reshape(N_SHARD, IMG_CAP, SEQ, D) * live
    grad_params, grad_tokens = pullback(grad_top)
    mixed = (outputs * live).reshape(SLOTS, SEQ, D).astype(jnp.bfloat16)
    token_grad = grad_tokens.reshape(SLOTS, SEQ, D).astype(jnp.bfloat16)
    return (mixed, token_grad, grad_params[0], grad_params[1], grad_params[2], grad_params[3], grad_params[4], grad_params[5], grad_params[6], grad_params[7], grad_params[8], grad_params[9], grad_params[10], grad_params[11])
```

```python
import functools

import jax
import jax.numpy as jnp
from jax import lax
from jax.sharding import PartitionSpec as P

HEAD = 64
EPSILON = 1e-06
LOW = jnp.bfloat16
WIDE = jnp.float32
SMALL = 128


def stages_of(count):
    found = []
    stride = 1
    while stride < count:
        radix = 4 if (count // stride) % 4 == 0 else 2
        found.append((stride, radix))
        stride *= radix
    return found[::-1]


def hop(array, count, offset):
    return lax.ppermute(array, "shard", [(i, i ^ offset) for i in range(count)])


def swap(array):
    return lax.ppermute(array, "tensor", [(0, 1), (1, 0)])


def pick(array, index, axis):
    return lax.dynamic_index_in_dim(array, index, axis, keepdims=False)


def gather_rows(piece, count, me):
    held = piece[None]
    for stride, radix in stages_of(count):
        digit = (me // stride) % radix
        got = [held] + [hop(held, count, k * stride) for k in range(1, radix)]
        stack = jnp.stack(got)
        held = jnp.stack([pick(stack, digit ^ a, 0) for a in range(radix)], axis=1)
        held = held.reshape((-1,) + piece.shape)
    return held


def scatter_rows(partial, count, me):
    held = partial
    for stride, radix in stages_of(count)[::-1]:
        digit = (me // stride) % radix
        view = held.reshape((-1, radix) + partial.shape[1:])
        total = pick(view, digit, 1)
        for k in range(1, radix):
            total = total + hop(pick(view, digit ^ k, 1).astype(LOW), count, k * stride).astype(WIDE)
        held = total
    return held[0]


def layer_stats(hidden):
    center = hidden - jnp.mean(hidden, -1, keepdims=True)
    inverse = lax.rsqrt(jnp.mean(center * center, -1, keepdims=True) + EPSILON)
    return (center * inverse, inverse)


def norm_back(grad_out, normal, inverse, gain):
    scaled = grad_out * gain
    return inverse * (
        scaled
        - jnp.mean(scaled, -1, keepdims=True)
        - normal * jnp.mean(scaled * normal, -1, keepdims=True)
    )


def project(inputs, weight):
    return jnp.einsum("csd,de->cse", inputs, weight, preferred_element_type=WIDE)


def back_project(grads, weight):
    return jnp.einsum("cse,de->csd", grads, weight, preferred_element_type=WIDE)


def weight_grad(inputs, grads):
    return jnp.einsum("csd,cse->de", inputs, grads, preferred_element_type=WIDE)


def token_sum(array):
    return jnp.sum(array, axis=(0, 1))


def pack_small(columns, rows, dtype):
    block = jnp.stack(columns, axis=-1).astype(dtype)
    return jnp.pad(block, [(0, 0)] * (block.ndim - 1) + [(0, SMALL - block.shape[-1])])


def body(shards, tokens, image_counts, input_weight, query_value_bias, output_weight, output_bias, first_gain,
         first_shift, second_gain, second_shift, expand_weight, expand_bias, reduce_weight, reduce_bias, cotangent):
    me = lax.axis_index("shard")
    core = lax.axis_index("tensor")
    rows, half = input_weight.shape[1:]
    units = expand_weight.shape[1]
    width = rows * shards
    small = pack_small(
        [first_gain, first_shift, second_gain, second_shift, output_bias, reduce_bias, query_value_bias.reshape(-1)]
        + list(expand_bias.reshape(-1, rows)), rows, LOW)
    first = jnp.concatenate([input_weight[0], input_weight[1], input_weight[2], output_weight.T, small], axis=1)
    second = jnp.concatenate([expand_weight, reduce_weight.T], axis=1)
    first = gather_rows(first, shards, me)
    second = gather_rows(second, shards, me)
    first_all = jnp.stack([first, swap(first)])
    second_all = jnp.stack([second, swap(second)])
    w_first = first_all.reshape(2, width, -1)
    w_second = second_all.reshape(2, width, -1)

    def both(block, start, size):
        return jnp.concatenate([block[0, :, start : start + size], block[1, :, start : start + size]], axis=1)

    wq, wk, wv, wo_t = (both(w_first, i * half, half) for i in range(4))
    w_expand = both(w_second, 0, units)
    w_reduce_t = both(w_second, units, units)
    tiny = first_all[..., 4 * half :].astype(WIDE)
    gain_one, shift_one, gain_two, shift_two, bias_out, bias_reduce = (tiny[0, :, :, i].reshape(-1) for i in range(6))
    bias_q = tiny[:, :, : rows // 2, 6].reshape(-1)
    bias_v = tiny[:, :, rows // 2 :, 6].reshape(-1)
    n_expand = units // width
    bias_expand = jnp.moveaxis(tiny[..., 7 : 7 + n_expand], -1, 2).reshape(-1)

    images = tokens.shape[0] // 2
    start = core * images
    tokens = lax.dynamic_slice_in_dim(tokens, start, images, 0)
    cotangent = lax.dynamic_slice_in_dim(cotangent, start, images, 0)
    slot_ids = start + jnp.arange(images, dtype=jnp.int32)
    live = (slot_ids < image_counts[0]).astype(WIDE)[:, None, None]
    hidden = tokens.astype(WIDE)
    length, features = hidden.shape[1:]
    head_shape = (images, length, features // HEAD, HEAD)
    flat = (images, length, features)
    normal_one, inverse_one = layer_stats(hidden)
    normed_one = (normal_one * gain_one + shift_one).astype(LOW)
    queries = ((project(normed_one, wq) + bias_q) * 0.125).astype(LOW).reshape(head_shape)
    key_rows = project(normed_one, wk).astype(LOW).reshape(head_shape)
    values = (project(normed_one, wv) + bias_v).astype(LOW).reshape(head_shape)
    scores = jnp.einsum("cqhe,ckhe->chqk", queries, key_rows, preferred_element_type=WIDE)
    attention = jax.nn.softmax(scores, axis=-1)
    weights_low = attention.astype(LOW)
    attended = jnp.einsum("chqk,ckhe->cqhe", weights_low, values, preferred_element_type=WIDE)
    attended = attended.astype(LOW).reshape(flat)
    middle = hidden + back_project(attended, wo_t) + bias_out
    normal_two, inverse_two = layer_stats(middle)
    normed_two = (normal_two * gain_two + shift_two).astype(LOW)
    before = project(normed_two, w_expand) + bias_expand
    activated, gelu_pull = jax.vjp(lambda value: jax.nn.gelu(value, approximate=False), before)
    activated_low = activated.astype(LOW)
    result = middle + back_project(activated_low, w_reduce_t) + bias_reduce
    mixed = (result * live).astype(LOW)

    grad_top = cotangent.astype(WIDE) * live
    grad_top_low = grad_top.astype(LOW)
    grad_reduce_bias = token_sum(grad_top)
    grad_reduce_t = weight_grad(grad_top_low, activated_low)
    grad_act = project(grad_top_low, w_reduce_t).astype(LOW).astype(WIDE)
    (grad_before,) = gelu_pull(grad_act)
    grad_before_low = grad_before.astype(LOW)
    grad_expand_bias = token_sum(grad_before_low.astype(WIDE))
    grad_expand = weight_grad(normed_two, grad_before_low)

    def finish(grad_mine_other):
        mine, other = grad_mine_other
        return scatter_rows(mine + swap(other.astype(LOW)).astype(WIDE), shards, me)

    def halves(array):
        cut = array.shape[-1] // 2
        return array[..., :cut], array[..., cut:]

    pairs = zip(halves(grad_expand), halves(grad_reduce_t))
    second_out = finish([jnp.concatenate(p, axis=1).reshape(shards, rows, -1) for p in pairs])

    grad_normed_two = back_project(grad_before_low, w_expand)
    grad_second_gain = token_sum(grad_normed_two * normal_two)
    grad_second_shift = token_sum(grad_normed_two)
    grad_middle = grad_top + norm_back(grad_normed_two, normal_two, inverse_two, gain_two)
    grad_output_bias = token_sum(grad_middle)
    grad_mid_low = grad_middle.astype(LOW)
    grad_output_t = weight_grad(grad_mid_low, attended)
    grad_attended = project(grad_mid_low, wo_t).astype(LOW).reshape(head_shape)
    grad_values = jnp.einsum("chqk,cqhe->ckhe", weights_low, grad_attended, preferred_element_type=WIDE).astype(LOW)
    grad_probs = jnp.einsum("cqhe,ckhe->chqk", grad_attended, values, preferred_element_type=WIDE)
    grad_scores = (attention * (grad_probs - jnp.sum(grad_probs * attention, -1, keepdims=True))).astype(LOW)
    grad_queries = jnp.einsum("chqk,ckhe->cqhe", grad_scores, key_rows, preferred_element_type=WIDE).astype(LOW)
    grad_keys = jnp.einsum("chqk,cqhe->ckhe", grad_scores, queries, preferred_element_type=WIDE).astype(LOW)
    grad_query_in = (grad_queries.astype(WIDE) * 0.125).astype(LOW).reshape(flat)
    grad_keys = grad_keys.reshape(flat)
    grad_values = grad_values.reshape(flat)
    grads_in = [weight_grad(normed_one, g) for g in (grad_query_in, grad_keys, grad_values)]
    grad_q_bias = token_sum(grad_query_in.astype(WIDE))
    grad_v_bias = token_sum(grad_values.astype(WIDE))
    grad_normed_one = (
        back_project(grad_query_in, wq) + back_project(grad_keys, wk) + back_project(grad_values, wv)
    )
    grad_first_gain = token_sum(grad_normed_one * normal_one)
    grad_first_shift = token_sum(grad_normed_one)
    token_grad = (grad_middle + norm_back(grad_normed_one, normal_one, inverse_one, gain_one)).astype(LOW)

    def small_block(i):
        shared = [grad_first_gain, grad_first_shift, grad_second_gain, grad_second_shift, grad_output_bias,
                  grad_reduce_bias]
        columns = [g.reshape(shards, rows) for g in shared]
        bias = [halves(g)[i].reshape(shards, rows // 2) for g in (grad_q_bias, grad_v_bias)]
        columns.append(jnp.concatenate(bias, axis=1))
        wide = halves(grad_expand_bias)[i].reshape(shards, n_expand, rows)
        columns += [wide[:, j] for j in range(n_expand)]
        return pack_small(columns, rows, WIDE)

    first_pairs = []
    for i in range(2):
        parts = [halves(g)[i].reshape(shards, rows, half) for g in grads_in + [grad_output_t]]
        first_pairs.append(jnp.concatenate(parts + [small_block(i)], axis=2))
    first_out = finish(first_pairs)

    def join(array):
        other = swap(array)
        return jnp.where(core == 0, jnp.concatenate([array, other]), jnp.concatenate([other, array]))

    tiny_out = first_out[:, 4 * half :]
    return (
        join(mixed),
        join(token_grad),
        jnp.stack([first_out[:, i * half : (i + 1) * half] for i in range(3)]),
        tiny_out[:, 6].reshape(2, 1, rows // 2),
        first_out[:, 3 * half : 4 * half].T,
        tiny_out[:, 4],
        tiny_out[:, 0],
        tiny_out[:, 1],
        tiny_out[:, 2],
        tiny_out[:, 3],
        second_out[:, :units],
        tiny_out[:, 7 : 7 + n_expand].T.reshape(1, -1),
        second_out[:, units:].T,
        tiny_out[:, 5],
    )


def solution(mesh):
    in_specs = (
        P("shard", None, None),
        P("shard"),
        P(None, "shard", "tensor"),
        P(None, "tensor", "shard"),
        P("tensor", "shard"),
        P("shard"),
        P("shard"),
        P("shard"),
        P("shard"),
        P("shard"),
        P("shard", "tensor"),
        P("tensor", "shard"),
        P("tensor", "shard"),
        P("shard"),
        P("shard", None, None),
    )
    out_specs = (
        P("shard", None, None),
        P("shard", None, None),
        P(None, "shard", "tensor"),
        P(None, "tensor", "shard"),
        P("tensor", "shard"),
        P("shard"),
        P("shard"),
        P("shard"),
        P("shard"),
        P("shard"),
        P("shard", "tensor"),
        P("tensor", "shard"),
        P("tensor", "shard"),
        P("shard"),
    )
    assert mesh.shape["tensor"] == 2
    return jax.shard_map(
        functools.partial(body, mesh.shape["shard"]), mesh=mesh, in_specs=in_specs, out_specs=out_specs, check_vma=False
    )
```

```python
import functools
import math

import jax
import jax.numpy as jnp
from jax import lax
from jax.experimental import pallas as pl
from jax.experimental.pallas import tpu as pltpu
from jax.sharding import PartitionSpec as P

HEAD = 64
EPSILON = 1e-06
LOW = jnp.bfloat16
WIDE = jnp.float32
SMALL = 128
VMEM_LIMIT = 60 * 1024 * 1024


def nn(a, b):
    return jnp.dot(a, b, preferred_element_type=WIDE)


def nt(a, b):
    return lax.dot_general(a, b, (((1,), (1,)), ((), ())), preferred_element_type=WIDE)


def tn(a, b):
    return lax.dot_general(a, b, (((0,), (0,)), ((), ())), preferred_element_type=WIDE)


def padded(length):
    return -(-length // 16) * 16


def stats(hidden):
    center = hidden - jnp.mean(hidden, -1, keepdims=True)
    inverse = lax.rsqrt(jnp.mean(center * center, -1, keepdims=True) + EPSILON)
    return center * inverse, inverse


def norm_back(grad_out, normal, inverse, gain):
    scaled = grad_out * gain
    return inverse * (
        scaled - jnp.mean(scaled, -1, keepdims=True) - normal * jnp.mean(scaled * normal, -1, keepdims=True)
    )


def selection(width, rows, period, offset, start, size, columns):
    row = lax.broadcasted_iota(jnp.int32, (width, columns), 0).astype(WIDE)
    column = lax.broadcasted_iota(jnp.int32, (width, columns), 1).astype(WIDE)
    shard = jnp.floor((row + 0.5) * (1.0 / rows))
    inner = row - shard * rows - start
    hit = (column == shard * period + offset + inner) & (inner >= 0.0) & (inner < size)
    return hit.astype(WIDE).astype(LOW)


def take(ref, at, count, stride):
    return jnp.concatenate([ref[c, pl.ds(at, count, stride=stride), :] for c in range(ref.shape[0])], axis=1)


def put(ref, at, stride, value):
    for c in range(ref.shape[0]):
        ref[c, pl.ds(at, value.shape[0], stride=stride), :] = value[:, c * SMALL : (c + 1) * SMALL]


def put_all(ref, value):
    for c in range(ref.shape[0]):
        ref[c, 0 : value.shape[0]] = value[:, c * SMALL : (c + 1) * SMALL]


def take_all(ref):
    return jnp.concatenate([ref[c] for c in range(ref.shape[0])], axis=1)


def attention_forward(
    rows, scalars, tokens, first, normed_out, qkv_out, probs_out, attended_out, middle_out, joined_out, hold, bias, wide
):
    width = first.shape[1]
    half = width // 2
    length, images = tokens.shape[:2]
    step = pl.program_id(0)

    @pl.when(step == 0)
    def _():
        hold[...] = jnp.zeros_like(hold)
        put_all(wide, tokens[...].astype(WIDE).reshape(length * images, width))
        spare = middle_out.shape[1] - length * images
        middle_out[:, length * images :] = jnp.zeros((middle_out.shape[0], spare, SMALL), WIDE)
        for i in range(4):
            joined_out[:, i * width : (i + 1) * width] = jnp.concatenate(
                [first[0, :, i * half : (i + 1) * half], first[1, :, i * half : (i + 1) * half]], axis=1
            )
        tiny = [first[i, :, 4 * half : 4 * half + SMALL] for i in range(2)]
        same = selection(width, rows, rows, 0, 0, rows, width)
        sel_q = selection(width, rows, rows // 2, 0, 0, rows // 2, half)
        sel_v = selection(width, rows, rows // 2, 0, rows // 2, rows // 2, half)
        shared = tn(tiny[0], same)
        bias[0:1, :width] = shared[0:1]
        bias[1:2, :width] = shared[1:2]
        bias[2:3, :width] = shared[4:5]
        zero = jnp.zeros((1, width), WIDE)
        b_q = jnp.concatenate([tn(t, sel_q)[6:7] for t in tiny], axis=1)
        b_v = jnp.concatenate([tn(t, sel_v)[6:7] for t in tiny], axis=1)
        bias[3:4] = jnp.concatenate([b_q, zero, b_v], axis=1)

    hold[0:length] = take(wide, step, length, images)
    hidden = hold[...]
    normal, _ = stats(hidden)
    normed = (normal * bias[0:1, :width] + bias[1:2, :width]).astype(LOW)
    normed_out[0] = normed
    projected = nn(normed, joined_out[:, : 3 * width]) + bias[3:4]
    queries = (projected[:, :width] * 0.125).astype(LOW)
    keys = projected[:, width : 2 * width].astype(LOW)
    values = projected[:, 2 * width :].astype(LOW)
    qkv_out[0, :, :width] = queries
    qkv_out[0, :, width : 2 * width] = keys
    qkv_out[0, :, 2 * width :] = values
    total = hidden.shape[0]
    lane = lax.broadcasted_iota(jnp.int32, (total, 2 * HEAD), 1)
    first_head = lane < HEAD
    valid = lax.broadcasted_iota(jnp.int32, (1, total), 1) < length
    for pair in range(width // (2 * HEAD)):
        cut = slice(pair * 2 * HEAD, (pair + 1) * 2 * HEAD)
        q_pair, k_pair, v_pair = queries[:, cut], keys[:, cut], values[:, cut]
        outs = []
        for e in range(2):
            mine = first_head if e == 0 else jnp.logical_not(first_head)
            q_one = jnp.where(mine, q_pair, jnp.zeros_like(q_pair))
            scores = jnp.where(valid, nt(q_one, k_pair), -1e30)
            top = jnp.max(scores, -1, keepdims=True)
            power = jnp.exp(scores - top)
            low = (power * (1.0 / jnp.sum(power, -1, keepdims=True))).astype(LOW)
            probs_out[0, 2 * pair + e] = low
            outs.append(nn(low, v_pair))
        attended_out[0, :, cut] = jnp.where(first_head, outs[0], outs[1]).astype(LOW)
    attended = attended_out[0]
    middle = hidden + nt(attended, joined_out[:, 3 * width :]) + bias[2:3, :width]
    put(middle_out, step, images, middle[:length])


def call_attention_forward(rows, scalars, tokens, first, images):
    length, _, width = tokens.shape
    total = padded(length)
    heads = width // HEAD
    flat = padded(length * images)

    def of_image(shape):
        return pl.BlockSpec((1,) + shape, lambda i, s: (i,) + (0,) * len(shape))

    shapes = [((total, width), LOW), ((total, 3 * width), LOW), ((heads, total, total), LOW), ((total, width), LOW)]
    return pl.pallas_call(
        functools.partial(attention_forward, rows),
        grid_spec=pltpu.PrefetchScalarGridSpec(
            num_scalar_prefetch=1,
            grid=(images,),
            in_specs=[
                pl.BlockSpec((length, images, width), lambda i, s: (0, s[0], 0), pipeline_mode=pl.Buffered(1)),
                pl.BlockSpec(first.shape, lambda i, s: (0, 0, 0), pipeline_mode=pl.Buffered(1)),
            ],
            out_specs=[of_image(s) for s, _ in shapes]
            + [pl.BlockSpec((width // SMALL, flat, SMALL), lambda i, s: (0, 0, 0)), pl.BlockSpec((width, 4 * width), lambda i, s: (0, 0))],
            scratch_shapes=[
                pltpu.VMEM((total, width), WIDE),
                pltpu.VMEM((8, 3 * width), WIDE),
                pltpu.VMEM((width // SMALL, length * images, SMALL), WIDE),
            ],
        ),
        out_shape=[jax.ShapeDtypeStruct((images,) + s, d) for s, d in shapes]
        + [jax.ShapeDtypeStruct((width // SMALL, flat, SMALL), WIDE), jax.ShapeDtypeStruct((width, 4 * width), LOW)],
        compiler_params=pltpu.CompilerParams(vmem_limit_bytes=VMEM_LIMIT),
        name="attention_forward",
    )(scalars, tokens, first)


def feed_forward(
    rows, chunk, length, scalars, middle, cotangent, first_small, second, mixed_out, grad_middle_out, own_out, other_out, sums_out,
    bias, own, other,
):
    width = second.shape[1]
    units = second.shape[2] // 2
    step = pl.program_id(0)
    block, images = cotangent.shape[:2]
    count = block * images

    @pl.when(step == 0)
    def _():
        own[...] = jnp.zeros_like(own)
        other[...] = jnp.zeros_like(other)
        sums_out[...] = jnp.zeros_like(sums_out)
        same = selection(width, rows, rows, 0, 0, rows, width)
        shared = tn(first_small[0], same)
        bias[0:1, :width] = shared[2:3]
        bias[1:2, :width] = shared[3:4]
        bias[2:3, :width] = shared[5:6]
        per = units // (width // rows)
        for i in range(2):
            line = jnp.zeros((1, units), WIDE)
            for c in range(per // rows):
                sel = selection(width, rows, per, c * rows, 0, rows, units)
                line = line + tn(first_small[i], sel)[7 + c : 8 + c]
            bias[3 + i : 4 + i, :units] = line

    gain = bias[0:1, :width]
    row = lax.broadcasted_iota(jnp.int32, (count, 1), 0)
    slot = scalars[0] * images + lax.rem(row, images)
    alive = slot < scalars[1]
    held = alive & (step * count + row < length * images)
    top = jnp.where(held, cotangent[...].astype(WIDE).reshape(count, width), 0.0)
    hidden = take_all(middle)
    normal, inverse = stats(hidden)
    normed = (normal * gain + bias[1:2, :width]).astype(LOW)
    top_low = top.astype(LOW)
    normed_t = normed.T
    top_t = top_low.T
    result = hidden + bias[2:3, :width]
    grad_normed = jnp.zeros_like(hidden)
    for i in range(2):
        grads = own if i == 0 else other
        for c in range(units // chunk):
            cut = slice(c * chunk, (c + 1) * chunk)
            cut_low = slice(units + c * chunk, units + (c + 1) * chunk)
            w_expand = second[i, :, cut]
            w_reduce = second[i, :, cut_low]
            before = nn(normed, w_expand) + bias[3 + i : 4 + i, cut]
            share = 0.5 + 0.5 * lax.erf(before * (1.0 / math.sqrt(2.0)))
            slope = share + before * jnp.exp(before * before * -0.5) * (1.0 / math.sqrt(2.0 * math.pi))
            active = (before * share).astype(LOW)
            result = result + nt(active, w_reduce)
            grad_act = nn(top_low, w_reduce).astype(LOW).astype(WIDE)
            grad_before = (grad_act * slope).astype(LOW)
            grad_normed = grad_normed + nt(grad_before, w_expand)
            grads[:, cut] += nn(normed_t, grad_before)
            grads[:, cut_low] += nn(top_t, active)
            sums_out[4 + i : 5 + i, cut] += jnp.sum(grad_before.astype(WIDE), 0, keepdims=True)
    mixed = jnp.where(alive, result, 0.0).reshape(block, images, width)
    mixed_out[...] = mixed.astype(LOW)
    grad_middle = top + norm_back(grad_normed, normal, inverse, gain)
    put_all(grad_middle_out, grad_middle)
    sums_out[0:1, :width] += jnp.sum(grad_normed * normal, 0, keepdims=True)
    sums_out[1:2, :width] += jnp.sum(grad_normed, 0, keepdims=True)
    sums_out[2:3, :width] += jnp.sum(grad_middle, 0, keepdims=True)
    sums_out[3:4, :width] += jnp.sum(top, 0, keepdims=True)

    @pl.when(step == pl.num_programs(0) - 1)
    def _():
        own_out[...] = own[...]
        other_out[...] = other[...].astype(LOW)


def call_feed_forward(rows, scalars, middle, cotangent, first, second, images, steps=3, chunk=256):
    length, _, width = cotangent.shape
    flat = middle.shape[1]
    columns = second.shape[2]
    block = flat // images // steps
    small_at = first.shape[2] // SMALL - 1
    return pl.pallas_call(
        functools.partial(feed_forward, rows, chunk, length),
        grid_spec=pltpu.PrefetchScalarGridSpec(
            num_scalar_prefetch=1,
            grid=(steps,),
            in_specs=[
                pl.BlockSpec((width // SMALL, block * images, SMALL), lambda i, s: (0, i, 0)),
                pl.BlockSpec((block, images, width), lambda i, s: (i, s[0], 0)),
                pl.BlockSpec((2, width, SMALL), lambda i, s: (0, 0, small_at), pipeline_mode=pl.Buffered(1)),
                pl.BlockSpec(second.shape, lambda i, s: (0, 0, 0), pipeline_mode=pl.Buffered(1)),
            ],
            out_specs=[
                pl.BlockSpec((block, images, width), lambda i, s: (i, 0, 0)),
                pl.BlockSpec((width // SMALL, block * images, SMALL), lambda i, s: (0, i, 0)),
                pl.BlockSpec((width, columns), lambda i, s: (0, 0)),
                pl.BlockSpec((width, columns), lambda i, s: (0, 0)),
                pl.BlockSpec((8, columns // 2), lambda i, s: (0, 0)),
            ],
            scratch_shapes=[
                pltpu.VMEM((8, columns // 2), WIDE),
                pltpu.VMEM((width, columns), WIDE),
                pltpu.VMEM((width, columns), WIDE),
            ],
        ),
        out_shape=[
            jax.ShapeDtypeStruct((length, images, width), LOW),
            jax.ShapeDtypeStruct((width // SMALL, flat, SMALL), WIDE),
            jax.ShapeDtypeStruct((width, columns), WIDE),
            jax.ShapeDtypeStruct((width, columns), LOW),
            jax.ShapeDtypeStruct((8, columns // 2), WIDE),
        ],
        compiler_params=pltpu.CompilerParams(vmem_limit_bytes=VMEM_LIMIT),
        name="feed_forward",
    )(scalars, middle, cotangent, first, second)


def attention_backward(
    rows, scalars, tokens, grad_middle, normed, qkv, probs, attended, joined, small, sums_in, token_out, own_out, other_out,
    hold, grads, grad_in, grad_out, sums, gain_row, wide, grads_wide,
):
    length, images, width = tokens.shape
    half = width // 2
    total = normed.shape[1]
    step = pl.program_id(0)

    @pl.when(step == 0)
    def _():
        hold[...] = jnp.zeros_like(hold)
        put_all(wide, tokens[...].astype(WIDE).reshape(length * images, width))
        grad_in[...] = jnp.zeros_like(grad_in)
        grad_out[...] = jnp.zeros_like(grad_out)
        sums[...] = jnp.zeros_like(sums)
        same = selection(width, rows, rows, 0, 0, rows, width)
        gain_row[0:1] = tn(small[0], same)[0:1]

    hold[0:length] = take(grad_middle, step, length, images)
    mid = hold[...]
    mid_low = mid.astype(LOW)
    grad_att = nn(mid_low, joined[:, 3 * width :]).astype(LOW)
    grad_out[...] += tn(mid_low, attended[0])
    lane = lax.broadcasted_iota(jnp.int32, (total, 2 * HEAD), 1)
    first_head = lane < HEAD
    for pair in range(width // (2 * HEAD)):
        cut = slice(pair * 2 * HEAD, (pair + 1) * 2 * HEAD)
        q_pair = qkv[0, :, cut]
        k_pair = qkv[0, :, width + pair * 2 * HEAD : width + (pair + 1) * 2 * HEAD]
        v_pair = qkv[0, :, 2 * width + pair * 2 * HEAD : 2 * width + (pair + 1) * 2 * HEAD]
        g_pair = grad_att[:, cut]
        g_values = g_queries = g_keys = None
        for e in range(2):
            mine = first_head if e == 0 else jnp.logical_not(first_head)
            zero = jnp.zeros_like(q_pair)
            low = probs[0, 2 * pair + e]
            g_one = jnp.where(mine, g_pair, zero)
            weight = low.astype(WIDE)
            slope = nt(g_one, v_pair)
            product = slope * weight
            g_scores = (product - weight * jnp.sum(product, -1, keepdims=True)).astype(LOW)
            parts = (
                tn(low, g_one),
                nn(g_scores, jnp.where(mine, k_pair, zero)),
                tn(g_scores, jnp.where(mine, q_pair, zero)),
            )
            g_values, g_queries, g_keys = (
                parts if e == 0 else (g_values + parts[0], g_queries + parts[1], g_keys + parts[2])
            )
        grads[:, cut] = g_queries.astype(LOW) * jnp.asarray(0.125, LOW)
        grads[:, width + pair * 2 * HEAD : width + (pair + 1) * 2 * HEAD] = g_keys.astype(LOW)
        grads[:, 2 * width + pair * 2 * HEAD : 2 * width + (pair + 1) * 2 * HEAD] = g_values.astype(LOW)
    grad_qkv = grads[...]
    grad_in[...] += tn(normed[0], grad_qkv)
    grad_normed = nt(grad_qkv, joined[:, : 3 * width])
    hold[0:length] = take(wide, step, length, images)
    normal, inverse = stats(hold[...])
    token_grad = mid + norm_back(grad_normed, normal, inverse, gain_row[0:1])
    put(grads_wide, step, images, token_grad[:length])
    sums[0:1, :width] += jnp.sum(grad_normed * normal, 0, keepdims=True)
    sums[1:2, :width] += jnp.sum(grad_normed, 0, keepdims=True)
    sums[2:3] += jnp.sum(grad_qkv.astype(WIDE), 0, keepdims=True)

    @pl.when(step == pl.num_programs(0) - 1)
    def _():
        token_out[...] = take_all(grads_wide).reshape(length, images, width).astype(LOW)
        units = sums_in.shape[1]
        same = selection(width, rows, rows, 0, 0, rows, width)
        sel_q = selection(width, rows, rows // 2, 0, 0, rows // 2, half)
        sel_v = selection(width, rows, rows // 2, 0, rows // 2, rows // 2, half)
        per = units // (width // rows)
        zero = jnp.zeros((1, width), WIDE)

        def lines(block, at, value):
            row = lax.broadcasted_iota(jnp.int32, (SMALL, value.shape[1]), 0)
            new = jnp.where(row == at, value, 0.0)
            return new if block is None else block + new

        shared = None
        for at, value in (
            (0, sums[0:1, :width]), (1, sums[1:2, :width]), (2, sums_in[0:1, :width]), (3, sums_in[1:2, :width]),
            (4, sums_in[2:3, :width]), (5, sums_in[3:4, :width]),
        ):
            shared = lines(shared, at, value)
        common = nt(same, shared.astype(LOW))
        for i in range(2):
            target = own_out if i == 0 else other_out
            for part in range(3):
                at = part * width + i * half
                target[:, part * half : (part + 1) * half] = grad_in[:, at : at + half].astype(target.dtype)
            target[:, 3 * half : 4 * half] = grad_out[:, i * half : (i + 1) * half].astype(target.dtype)
            tiny = common
            tiny = tiny + nt(sel_q, lines(None, 6, sums[2:3, i * half : (i + 1) * half]).astype(LOW))
            tiny = tiny + nt(sel_v, lines(None, 6, sums[2:3, 2 * width + i * half : 2 * width + (i + 1) * half]).astype(LOW))
            for c in range(per // rows):
                sel = selection(width, rows, per, c * rows, 0, rows, units)
                tiny = tiny + nt(sel, lines(None, 7 + c, sums_in[4 + i : 5 + i]).astype(LOW))
            target[:, 4 * half :] = tiny.astype(target.dtype)


def call_attention_backward(rows, scalars, tokens, grad_middle, normed, qkv, probs, attended, joined, first, sums_in, images):
    length, _, width = tokens.shape
    total = normed.shape[1]
    columns = first.shape[2]
    small_at = columns // SMALL - 1

    def of_image(array):
        return pl.BlockSpec((1,) + array.shape[1:], lambda i, s: (i,) + (0,) * (array.ndim - 1))

    def whole(array):
        return pl.BlockSpec(array.shape, lambda i, s: (0,) * array.ndim, pipeline_mode=pl.Buffered(1))

    return pl.pallas_call(
        functools.partial(attention_backward, rows),
        grid_spec=pltpu.PrefetchScalarGridSpec(
            num_scalar_prefetch=1,
            grid=(images,),
            in_specs=[
                pl.BlockSpec((length, images, width), lambda i, s: (0, s[0], 0), pipeline_mode=pl.Buffered(1)),
                whole(grad_middle), of_image(normed), of_image(qkv), of_image(probs), of_image(attended),
                whole(joined),
                pl.BlockSpec((2, width, SMALL), lambda i, s: (0, 0, small_at), pipeline_mode=pl.Buffered(1)),
                whole(sums_in),
            ],
            out_specs=[
                pl.BlockSpec((length, images, width), lambda i, s: (0, 0, 0)),
                pl.BlockSpec((width, columns), lambda i, s: (0, 0)),
                pl.BlockSpec((width, columns), lambda i, s: (0, 0)),
            ],
            scratch_shapes=[
                pltpu.VMEM((total, width), WIDE),
                pltpu.VMEM((total, 3 * width), LOW),
                pltpu.VMEM((width, 3 * width), WIDE),
                pltpu.VMEM((width, width), WIDE),
                pltpu.VMEM((8, 3 * width), WIDE),
                pltpu.VMEM((8, width), WIDE),
                pltpu.VMEM((width // SMALL, length * images, SMALL), WIDE),
                pltpu.VMEM((width // SMALL, length * images, SMALL), WIDE),
            ],
        ),
        out_shape=[
            jax.ShapeDtypeStruct((length, images, width), LOW),
            jax.ShapeDtypeStruct((width, columns), WIDE),
            jax.ShapeDtypeStruct((width, columns), LOW),
        ],
        compiler_params=pltpu.CompilerParams(vmem_limit_bytes=VMEM_LIMIT),
        name="attention_backward",
    )(scalars, tokens, grad_middle, normed, qkv, probs, attended, joined, first, sums_in)


def stages_of(count):
    found = []
    stride = 1
    while stride < count:
        radix = 4 if (count // stride) % 4 == 0 else 2
        found.append((stride, radix))
        stride *= radix
    return found[::-1]


def hop(array, count, offset):
    return lax.ppermute(array, "shard", [(i, i ^ offset) for i in range(count)])


def swap(array):
    return lax.ppermute(array, "tensor", [(0, 1), (1, 0)])


def gather_pieces(piece, count):
    held, owners = piece[None], [0]
    levels = stages_of(count)
    for at, (stride, radix) in enumerate(levels):
        got = [held] + [hop(held, count, k * stride) for k in range(1, radix)]
        marks = [[o ^ (k * stride) for o in owners] for k in range(radix)]
        if at + 1 < len(levels):
            held, owners = jnp.concatenate(got), sum(marks, [])
    return got, marks


def assemble(scalars, got, marks, count):
    arrays = got + [swap(g) for g in got]
    places = [(half, a, b, mark) for half in range(2) for a, line in enumerate(marks) for b, mark in enumerate(line)]

    def kernel(scalars, *refs):
        ins, out, sems = refs[: len(arrays)], refs[-2], refs[-1]
        copies = []
        for at, (half, a, b, mark) in enumerate(places):
            owner = lax.bitwise_xor(scalars[2], mark)
            source = ins[half * len(got) + a].at[b]
            copies.append(pltpu.make_async_copy(source, out.at[half, owner], sems.at[at]))
        for copy in copies:
            copy.start()
        for copy in copies:
            copy.wait()

    shape = (2, count) + got[0].shape[1:]
    anywhere = pl.BlockSpec(memory_space=pl.ANY)
    return pl.pallas_call(
        kernel,
        in_specs=[pl.BlockSpec(memory_space=pltpu.SMEM)] + [anywhere] * len(arrays),
        out_specs=anywhere,
        scratch_shapes=[pltpu.SemaphoreType.DMA((len(places),))],
        out_shape=jax.ShapeDtypeStruct(shape, LOW),
        name="assemble",
    )(scalars, *arrays)


def combine(scalars, arrays, stride, radix):
    blocks, rows, columns = arrays[0].shape
    high = blocks // radix

    def kernel(scalars, *refs):
        outs = refs[len(arrays) * radix :]
        for k in range(radix):
            total = None
            for a in range(len(arrays)):
                value = refs[a * radix + k][0].astype(WIDE)
                total = value if total is None else total + value
            outs[k][0] = total.astype(outs[k].dtype)

    def block(k):
        def index(i, s):
            return (i * radix + (lax.rem(lax.div(s[2], stride), radix) ^ k), 0, 0)

        return pl.BlockSpec((1, rows, columns), index)

    return pl.pallas_call(
        kernel,
        grid_spec=pltpu.PrefetchScalarGridSpec(
            num_scalar_prefetch=1,
            grid=(high,),
            in_specs=[block(k) for _ in arrays for k in range(radix)],
            out_specs=[pl.BlockSpec((1, rows, columns), lambda i, s: (i, 0, 0))] * radix,
        ),
        out_shape=[jax.ShapeDtypeStruct((high, rows, columns), LOW if k else WIDE) for k in range(radix)],
        name="combine",
    )(scalars, *[a for a in arrays for _ in range(radix)])


def scatter_rows(scalars, own, received, count):
    arrays = [own, received]
    for stride, radix in stages_of(count)[::-1]:
        sums = combine(scalars, arrays, stride, radix)
        arrays = [sums[0]] + [hop(sums[k], count, k * stride) for k in range(1, radix)]
    return arrays


def total_of(refs):
    total = refs[0][0]
    for ref in refs[1:]:
        total = total + ref[0].astype(WIDE)
    return total


def finish_second(arrays, units):
    rows = arrays[0].shape[1]

    def kernel(*refs):
        total = total_of(refs[:-2])
        refs[-2][...] = total[:, :units]
        refs[-1][...] = total[:, units:]

    return pl.pallas_call(
        kernel, out_shape=[jax.ShapeDtypeStruct((rows, units), WIDE)] * 2, name="finish_second"
    )(*arrays)


def finish_first(arrays, half, units):
    rows = arrays[0].shape[1]
    per = units // (2 * half // rows)

    def kernel(*refs):
        outs = refs[len(arrays) :]
        total = total_of(refs[: len(arrays)])
        for i in range(3):
            outs[0][i] = total[:, i * half : (i + 1) * half]
        outs[1][...] = total[:, 3 * half : 4 * half]
        tiny = total[:, 4 * half :]

        def line(at, start, size, columns, shift):
            row = lax.broadcasted_iota(jnp.int32, (rows, columns), 0) - start
            lane = lax.broadcasted_iota(jnp.int32, (rows, columns), 1) - shift
            hit = (row == lane) & (row >= 0) & (row < size)
            return jnp.sum(jnp.where(hit, tiny[:, at : at + 1], 0.0), 0, keepdims=True)

        for i in range(6):
            outs[2 + i][...] = line(i, 0, rows, rows, 0)
        for i in range(2):
            outs[8][i] = line(6, i * (rows // 2), rows // 2, rows // 2, 0)
        wide = line(7, 0, rows, per, 0)
        for c in range(1, per // rows):
            wide = wide + line(7 + c, 0, rows, per, c * rows)
        outs[9][...] = wide

    shapes = [(3, rows, half), (rows, half)] + [(1, rows)] * 6 + [(2, 1, rows // 2), (1, per)]
    return pl.pallas_call(
        kernel, out_shape=[jax.ShapeDtypeStruct(s, WIDE) for s in shapes], name="finish_first"
    )(*arrays)


def join(scalars, array):
    length, images, width = array.shape
    other = swap(array)

    def kernel(scalars, own, other, out, sems):
        here = pltpu.make_async_copy(own, out.at[:, scalars[0]], sems.at[0])
        there = pltpu.make_async_copy(other, out.at[:, 1 - scalars[0]], sems.at[1])
        here.start()
        there.start()
        here.wait()
        there.wait()

    anywhere = pl.BlockSpec(memory_space=pl.ANY)
    out = pl.pallas_call(
        kernel,
        in_specs=[pl.BlockSpec(memory_space=pltpu.SMEM), anywhere, anywhere],
        out_specs=anywhere,
        scratch_shapes=[pltpu.SemaphoreType.DMA((2,))],
        out_shape=jax.ShapeDtypeStruct((length, 2, images, width), array.dtype),
        name="join",
    )(scalars, array, other)
    return out.reshape(length, 2 * images, width).transpose(1, 0, 2)


def pack_small(columns):
    block = jnp.stack(columns, axis=-1)
    return jnp.pad(block, [(0, 0), (0, SMALL - block.shape[-1])])


def body(shards, tokens, image_counts, input_weight, query_value_bias, output_weight, output_bias, first_gain,
         first_shift, second_gain, second_shift, expand_weight, expand_bias, reduce_weight, reduce_bias, cotangent):
    rows, half = input_weight.shape[1:]
    units = expand_weight.shape[1]
    width = rows * shards
    images = tokens.shape[0] // 2
    scalars = jnp.stack([lax.axis_index("tensor"), image_counts[0], lax.axis_index("shard")]).astype(jnp.int32)
    small = pack_small(
        [first_gain, first_shift, second_gain, second_shift, output_bias, reduce_bias, query_value_bias.reshape(-1)]
        + list(expand_bias.reshape(-1, rows)))
    first = jnp.concatenate([input_weight[0], input_weight[1], input_weight[2], output_weight.T, small], axis=1)
    second = jnp.concatenate([expand_weight, reduce_weight.T], axis=1)
    first = assemble(scalars, *gather_pieces(first, shards), shards).reshape(2, width, -1)
    second = assemble(scalars, *gather_pieces(second, shards), shards).reshape(2, width, -1)
    tokens = tokens.transpose(1, 0, 2)
    cotangent = cotangent.transpose(1, 0, 2)
    normed, qkv, probs, attended, middle, joined = call_attention_forward(rows, scalars, tokens, first, images)
    mixed, grad_middle, own, other, sums = call_feed_forward(rows, scalars, middle, cotangent, first, second, images)

    def spread(own, other):
        shape = (shards, rows, -1)
        return scatter_rows(scalars, own.reshape(shape), swap(other).reshape(shape), shards)

    grad_expand, grad_reduce = finish_second(spread(own, other), units)
    token_grad, own, other = call_attention_backward(
        rows, scalars, tokens, grad_middle, normed, qkv, probs, attended, joined, first, sums, images)
    outs = finish_first(spread(own, other), half, units)
    gains = [o.reshape(rows) for o in outs[2:8]]
    return (
        join(scalars, mixed),
        join(scalars, token_grad),
        outs[0],
        outs[8],
        outs[1].T,
        gains[4],
        gains[0],
        gains[1],
        gains[2],
        gains[3],
        grad_expand,
        outs[9],
        grad_reduce.T,
        gains[5],
    )


def solution(mesh):
    in_specs = (
        P("shard", None, None),
        P("shard"),
        P(None, "shard", "tensor"),
        P(None, "tensor", "shard"),
        P("tensor", "shard"),
        P("shard"),
        P("shard"),
        P("shard"),
        P("shard"),
        P("shard"),
        P("shard", "tensor"),
        P("tensor", "shard"),
        P("tensor", "shard"),
        P("shard"),
        P("shard", None, None),
    )
    out_specs = in_specs[:1] + in_specs[-1:] + in_specs[2:-1]
    assert mesh.shape["tensor"] == 2
    return jax.shard_map(
        functools.partial(body, mesh.shape["shard"]), mesh=mesh, in_specs=in_specs, out_specs=out_specs, check_vma=False
    )
```

```python
import functools
import math

import jax
import jax.numpy as jnp
from jax import lax
from jax.experimental import pallas as pl
from jax.experimental.pallas import tpu as pltpu
from jax.sharding import PartitionSpec as P

HEAD = 64
EPSILON = 1e-06
LOW = jnp.bfloat16
WIDE = jnp.float32
SMALL = 128
VMEM_LIMIT = 32 * 1024 * 1024
SMALL_LIMIT = 16 * 1024 * 1024


def nn(a, b):
    return jnp.dot(a, b, preferred_element_type=WIDE)


def nt(a, b):
    return lax.dot_general(a, b, (((1,), (1,)), ((), ())), preferred_element_type=WIDE)


def tn(a, b):
    return lax.dot_general(a, b, (((0,), (0,)), ((), ())), preferred_element_type=WIDE)


def padded(length):
    return -(-length // 16) * 16


def stats(hidden):
    center = hidden - jnp.mean(hidden, -1, keepdims=True)
    inverse = lax.rsqrt(jnp.mean(center * center, -1, keepdims=True) + EPSILON)
    return center * inverse, inverse


def norm_back(grad_out, normal, inverse, gain):
    scaled = grad_out * gain
    return inverse * (
        scaled - jnp.mean(scaled, -1, keepdims=True) - normal * jnp.mean(scaled * normal, -1, keepdims=True)
    )


def selection(width, rows, period, offset, start, size, columns):
    row = lax.broadcasted_iota(jnp.int32, (width, columns), 0).astype(WIDE)
    column = lax.broadcasted_iota(jnp.int32, (width, columns), 1).astype(WIDE)
    shard = jnp.floor((row + 0.5) * (1.0 / rows))
    inner = row - shard * rows - start
    hit = (column == shard * period + offset + inner) & (inner >= 0.0) & (inner < size)
    return hit.astype(WIDE).astype(LOW)


def take(ref, at, count, stride):
    return jnp.concatenate([ref[c, pl.ds(at, count, stride=stride), :] for c in range(ref.shape[0])], axis=1)


def put(ref, at, stride, value):
    for c in range(ref.shape[0]):
        ref[c, pl.ds(at, value.shape[0], stride=stride), :] = value[:, c * SMALL : (c + 1) * SMALL]


def put_all(ref, value):
    for c in range(ref.shape[0]):
        ref[c, 0 : value.shape[0]] = value[:, c * SMALL : (c + 1) * SMALL]


def take_all(ref):
    return jnp.concatenate([ref[c] for c in range(ref.shape[0])], axis=1)


def attention_forward(
    rows, scalars, tokens, first, normed_out, qkv_out, probs_out, attended_out, middle_out, joined_out, hold, bias, wide
):
    width = first.shape[1]
    half = width // 2
    length, images = tokens.shape[:2]
    step = pl.program_id(0)

    @pl.when(step == 0)
    def _():
        hold[...] = jnp.zeros_like(hold)
        put_all(wide, tokens[...].astype(WIDE).reshape(length * images, width))
        spare = middle_out.shape[1] - length * images
        middle_out[:, length * images :] = jnp.zeros((middle_out.shape[0], spare, SMALL), WIDE)
        for i in range(4):
            joined_out[:, i * width : (i + 1) * width] = jnp.concatenate(
                [first[0, :, i * half : (i + 1) * half], first[1, :, i * half : (i + 1) * half]], axis=1
            )
        tiny = [first[i, :, 4 * half : 4 * half + SMALL] for i in range(2)]
        same = selection(width, rows, rows, 0, 0, rows, width)
        sel_q = selection(width, rows, rows // 2, 0, 0, rows // 2, half)
        sel_v = selection(width, rows, rows // 2, 0, rows // 2, rows // 2, half)
        shared = tn(tiny[0], same)
        bias[0:1, :width] = shared[0:1]
        bias[1:2, :width] = shared[1:2]
        bias[2:3, :width] = shared[4:5]
        zero = jnp.zeros((1, width), WIDE)
        b_q = jnp.concatenate([tn(t, sel_q)[6:7] for t in tiny], axis=1)
        b_v = jnp.concatenate([tn(t, sel_v)[6:7] for t in tiny], axis=1)
        bias[3:4] = jnp.concatenate([b_q, zero, b_v], axis=1)

    hold[0:length] = take(wide, step, length, images)
    hidden = hold[...]
    normal, _ = stats(hidden)
    normed = (normal * bias[0:1, :width] + bias[1:2, :width]).astype(LOW)
    normed_out[0] = normed
    projected = nn(normed, joined_out[:, : 3 * width]) + bias[3:4]
    queries = (projected[:, :width] * 0.125).astype(LOW)
    keys = projected[:, width : 2 * width].astype(LOW)
    values = projected[:, 2 * width :].astype(LOW)
    qkv_out[0, :, :width] = queries
    qkv_out[0, :, width : 2 * width] = keys
    qkv_out[0, :, 2 * width :] = values
    total = hidden.shape[0]
    lane = lax.broadcasted_iota(jnp.int32, (total, 2 * HEAD), 1)
    first_head = lane < HEAD
    valid = lax.broadcasted_iota(jnp.int32, (1, total), 1) < length
    for pair in range(width // (2 * HEAD)):
        cut = slice(pair * 2 * HEAD, (pair + 1) * 2 * HEAD)
        q_pair, k_pair, v_pair = queries[:, cut], keys[:, cut], values[:, cut]
        outs = []
        for e in range(2):
            mine = first_head if e == 0 else jnp.logical_not(first_head)
            q_one = jnp.where(mine, q_pair, jnp.zeros_like(q_pair))
            scores = jnp.where(valid, nt(q_one, k_pair), -1e30)
            top = jnp.max(scores, -1, keepdims=True)
            power = jnp.exp(scores - top)
            low = (power * (1.0 / jnp.sum(power, -1, keepdims=True))).astype(LOW)
            probs_out[0, 2 * pair + e] = low
            outs.append(nn(low, v_pair))
        attended_out[0, :, cut] = jnp.where(first_head, outs[0], outs[1]).astype(LOW)
    attended = attended_out[0]
    middle = hidden + nt(attended, joined_out[:, 3 * width :]) + bias[2:3, :width]
    put(middle_out, step, images, middle[:length])


def call_attention_forward(rows, scalars, tokens, first, images):
    length, _, width = tokens.shape
    total = padded(length)
    heads = width // HEAD
    flat = padded(length * images)

    def of_image(shape):
        return pl.BlockSpec((1,) + shape, lambda i, s: (i,) + (0,) * len(shape))

    shapes = [((total, width), LOW), ((total, 3 * width), LOW), ((heads, total, total), LOW), ((total, width), LOW)]
    return pl.pallas_call(
        functools.partial(attention_forward, rows),
        grid_spec=pltpu.PrefetchScalarGridSpec(
            num_scalar_prefetch=1,
            grid=(images,),
            in_specs=[
                pl.BlockSpec((length, images, width), lambda i, s: (0, s[0], 0), pipeline_mode=pl.Buffered(1)),
                pl.BlockSpec(first.shape, lambda i, s: (0, 0, 0), pipeline_mode=pl.Buffered(1)),
            ],
            out_specs=[of_image(s) for s, _ in shapes]
            + [pl.BlockSpec((width // SMALL, flat, SMALL), lambda i, s: (0, 0, 0)), pl.BlockSpec((width, 4 * width), lambda i, s: (0, 0))],
            scratch_shapes=[
                pltpu.VMEM((total, width), WIDE),
                pltpu.VMEM((8, 3 * width), WIDE),
                pltpu.VMEM((width // SMALL, length * images, SMALL), WIDE),
            ],
        ),
        out_shape=[jax.ShapeDtypeStruct((images,) + s, d) for s, d in shapes]
        + [jax.ShapeDtypeStruct((width // SMALL, flat, SMALL), WIDE), jax.ShapeDtypeStruct((width, 4 * width), LOW)],
        compiler_params=pltpu.CompilerParams(vmem_limit_bytes=VMEM_LIMIT),
        name="attention_forward",
    )(scalars, tokens, first)


def feed_forward(
    rows, chunk, length, scalars, middle, cotangent, first_small, second, mixed_out, grad_middle_out, own_out, other_out, sums_out,
    bias, own, other,
):
    width = second.shape[1]
    units = second.shape[2] // 2
    step = pl.program_id(0)
    block, images = cotangent.shape[:2]
    count = block * images

    @pl.when(step == 0)
    def _():
        own[...] = jnp.zeros_like(own)
        other[...] = jnp.zeros_like(other)
        sums_out[...] = jnp.zeros_like(sums_out)
        same = selection(width, rows, rows, 0, 0, rows, width)
        shared = tn(first_small[0], same)
        bias[0:1, :width] = shared[2:3]
        bias[1:2, :width] = shared[3:4]
        bias[2:3, :width] = shared[5:6]
        per = units // (width // rows)
        for i in range(2):
            line = jnp.zeros((1, units), WIDE)
            for c in range(per // rows):
                sel = selection(width, rows, per, c * rows, 0, rows, units)
                line = line + tn(first_small[i], sel)[7 + c : 8 + c]
            bias[3 + i : 4 + i, :units] = line

    gain = bias[0:1, :width]
    row = lax.broadcasted_iota(jnp.int32, (count, 1), 0)
    slot = scalars[0] * images + lax.rem(row, images)
    alive = slot < scalars[1]
    held = alive & (step * count + row < length * images)
    top = jnp.where(held, cotangent[...].astype(WIDE).reshape(count, width), 0.0)
    hidden = take_all(middle)
    normal, inverse = stats(hidden)
    normed = (normal * gain + bias[1:2, :width]).astype(LOW)
    top_low = top.astype(LOW)
    normed_t = normed.T
    top_t = top_low.T
    result = hidden + bias[2:3, :width]
    grad_normed = jnp.zeros_like(hidden)
    for i in range(2):
        grads = own if i == 0 else other
        for c in range(units // chunk):
            cut = slice(c * chunk, (c + 1) * chunk)
            cut_low = slice(units + c * chunk, units + (c + 1) * chunk)
            w_expand = second[i, :, cut]
            w_reduce = second[i, :, cut_low]
            before = nn(normed, w_expand) + bias[3 + i : 4 + i, cut]
            share = 0.5 + 0.5 * lax.erf(before * (1.0 / math.sqrt(2.0)))
            slope = share + before * jnp.exp(before * before * -0.5) * (1.0 / math.sqrt(2.0 * math.pi))
            active = (before * share).astype(LOW)
            result = result + nt(active, w_reduce)
            grad_act = nn(top_low, w_reduce).astype(LOW).astype(WIDE)
            grad_before = (grad_act * slope).astype(LOW)
            grad_normed = grad_normed + nt(grad_before, w_expand)
            grads[:, cut] += nn(normed_t, grad_before)
            grads[:, cut_low] += nn(top_t, active)
            sums_out[4 + i : 5 + i, cut] += jnp.sum(grad_before.astype(WIDE), 0, keepdims=True)
    mixed = jnp.where(alive, result, 0.0).reshape(block, images, width)
    mixed_out[...] = mixed.astype(LOW)
    grad_middle = top + norm_back(grad_normed, normal, inverse, gain)
    put_all(grad_middle_out, grad_middle)
    sums_out[0:1, :width] += jnp.sum(grad_normed * normal, 0, keepdims=True)
    sums_out[1:2, :width] += jnp.sum(grad_normed, 0, keepdims=True)
    sums_out[2:3, :width] += jnp.sum(grad_middle, 0, keepdims=True)
    sums_out[3:4, :width] += jnp.sum(top, 0, keepdims=True)

    @pl.when(step == pl.num_programs(0) - 1)
    def _():
        own_out[...] = own[...]
        other_out[...] = other[...].astype(LOW)


def call_feed_forward(rows, scalars, middle, cotangent, first, second, images, steps=3, chunk=256):
    length, _, width = cotangent.shape
    flat = middle.shape[1]
    columns = second.shape[2]
    block = flat // images // steps
    small_at = first.shape[2] // SMALL - 1
    return pl.pallas_call(
        functools.partial(feed_forward, rows, chunk, length),
        grid_spec=pltpu.PrefetchScalarGridSpec(
            num_scalar_prefetch=1,
            grid=(steps,),
            in_specs=[
                pl.BlockSpec((width // SMALL, block * images, SMALL), lambda i, s: (0, i, 0)),
                pl.BlockSpec((block, images, width), lambda i, s: (i, s[0], 0)),
                pl.BlockSpec((2, width, SMALL), lambda i, s: (0, 0, small_at), pipeline_mode=pl.Buffered(1)),
                pl.BlockSpec(second.shape, lambda i, s: (0, 0, 0), pipeline_mode=pl.Buffered(1)),
            ],
            out_specs=[
                pl.BlockSpec((block, images, width), lambda i, s: (i, 0, 0)),
                pl.BlockSpec((width // SMALL, block * images, SMALL), lambda i, s: (0, i, 0)),
                pl.BlockSpec((width, columns), lambda i, s: (0, 0)),
                pl.BlockSpec((width, columns), lambda i, s: (0, 0)),
                pl.BlockSpec((8, columns // 2), lambda i, s: (0, 0)),
            ],
            scratch_shapes=[
                pltpu.VMEM((8, columns // 2), WIDE),
                pltpu.VMEM((width, columns), WIDE),
                pltpu.VMEM((width, columns), WIDE),
            ],
        ),
        out_shape=[
            jax.ShapeDtypeStruct((length, images, width), LOW),
            jax.ShapeDtypeStruct((width // SMALL, flat, SMALL), WIDE),
            jax.ShapeDtypeStruct((width, columns), WIDE),
            jax.ShapeDtypeStruct((width, columns), LOW),
            jax.ShapeDtypeStruct((8, columns // 2), WIDE),
        ],
        compiler_params=pltpu.CompilerParams(vmem_limit_bytes=VMEM_LIMIT),
        name="feed_forward",
    )(scalars, middle, cotangent, first, second)


def attention_backward(
    rows, scalars, tokens, grad_middle, normed, qkv, probs, attended, joined, small, sums_in, token_out, own_out, other_out,
    hold, grads, grad_in, grad_out, sums, gain_row, wide, grads_wide,
):
    length, images, width = tokens.shape
    half = width // 2
    total = normed.shape[1]
    step = pl.program_id(0)

    @pl.when(step == 0)
    def _():
        hold[...] = jnp.zeros_like(hold)
        put_all(wide, tokens[...].astype(WIDE).reshape(length * images, width))
        grad_in[...] = jnp.zeros_like(grad_in)
        grad_out[...] = jnp.zeros_like(grad_out)
        sums[...] = jnp.zeros_like(sums)
        same = selection(width, rows, rows, 0, 0, rows, width)
        gain_row[0:1] = tn(small[0], same)[0:1]

    hold[0:length] = take(grad_middle, step, length, images)
    mid = hold[...]
    mid_low = mid.astype(LOW)
    grad_att = nn(mid_low, joined[:, 3 * width :]).astype(LOW)
    grad_out[...] += tn(mid_low, attended[0])
    lane = lax.broadcasted_iota(jnp.int32, (total, 2 * HEAD), 1)
    first_head = lane < HEAD
    for pair in range(width // (2 * HEAD)):
        cut = slice(pair * 2 * HEAD, (pair + 1) * 2 * HEAD)
        q_pair = qkv[0, :, cut]
        k_pair = qkv[0, :, width + pair * 2 * HEAD : width + (pair + 1) * 2 * HEAD]
        v_pair = qkv[0, :, 2 * width + pair * 2 * HEAD : 2 * width + (pair + 1) * 2 * HEAD]
        g_pair = grad_att[:, cut]
        g_values = g_queries = g_keys = None
        for e in range(2):
            mine = first_head if e == 0 else jnp.logical_not(first_head)
            zero = jnp.zeros_like(q_pair)
            low = probs[0, 2 * pair + e]
            g_one = jnp.where(mine, g_pair, zero)
            weight = low.astype(WIDE)
            slope = nt(g_one, v_pair)
            product = slope * weight
            g_scores = (product - weight * jnp.sum(product, -1, keepdims=True)).astype(LOW)
            parts = (
                tn(low, g_one),
                nn(g_scores, jnp.where(mine, k_pair, zero)),
                tn(g_scores, jnp.where(mine, q_pair, zero)),
            )
            g_values, g_queries, g_keys = (
                parts if e == 0 else (g_values + parts[0], g_queries + parts[1], g_keys + parts[2])
            )
        grads[:, cut] = g_queries.astype(LOW) * jnp.asarray(0.125, LOW)
        grads[:, width + pair * 2 * HEAD : width + (pair + 1) * 2 * HEAD] = g_keys.astype(LOW)
        grads[:, 2 * width + pair * 2 * HEAD : 2 * width + (pair + 1) * 2 * HEAD] = g_values.astype(LOW)
    grad_qkv = grads[...]
    grad_in[...] += tn(normed[0], grad_qkv)
    grad_normed = nt(grad_qkv, joined[:, : 3 * width])
    hold[0:length] = take(wide, step, length, images)
    normal, inverse = stats(hold[...])
    token_grad = mid + norm_back(grad_normed, normal, inverse, gain_row[0:1])
    put(grads_wide, step, images, token_grad[:length])
    sums[0:1, :width] += jnp.sum(grad_normed * normal, 0, keepdims=True)
    sums[1:2, :width] += jnp.sum(grad_normed, 0, keepdims=True)
    sums[2:3] += jnp.sum(grad_qkv.astype(WIDE), 0, keepdims=True)

    @pl.when(step == pl.num_programs(0) - 1)
    def _():
        token_out[...] = take_all(grads_wide).reshape(length, images, width).astype(LOW)
        units = sums_in.shape[1]
        same = selection(width, rows, rows, 0, 0, rows, width)
        sel_q = selection(width, rows, rows // 2, 0, 0, rows // 2, half)
        sel_v = selection(width, rows, rows // 2, 0, rows // 2, rows // 2, half)
        per = units // (width // rows)
        zero = jnp.zeros((1, width), WIDE)

        def lines(block, at, value):
            row = lax.broadcasted_iota(jnp.int32, (SMALL, value.shape[1]), 0)
            new = jnp.where(row == at, value, 0.0)
            return new if block is None else block + new

        shared = None
        for at, value in (
            (0, sums[0:1, :width]), (1, sums[1:2, :width]), (2, sums_in[0:1, :width]), (3, sums_in[1:2, :width]),
            (4, sums_in[2:3, :width]), (5, sums_in[3:4, :width]),
        ):
            shared = lines(shared, at, value)
        common = nt(same, shared.astype(LOW))
        for i in range(2):
            target = own_out if i == 0 else other_out
            for part in range(3):
                at = part * width + i * half
                target[:, part * half : (part + 1) * half] = grad_in[:, at : at + half].astype(target.dtype)
            target[:, 3 * half : 4 * half] = grad_out[:, i * half : (i + 1) * half].astype(target.dtype)
            tiny = common
            tiny = tiny + nt(sel_q, lines(None, 6, sums[2:3, i * half : (i + 1) * half]).astype(LOW))
            tiny = tiny + nt(sel_v, lines(None, 6, sums[2:3, 2 * width + i * half : 2 * width + (i + 1) * half]).astype(LOW))
            for c in range(per // rows):
                sel = selection(width, rows, per, c * rows, 0, rows, units)
                tiny = tiny + nt(sel, lines(None, 7 + c, sums_in[4 + i : 5 + i]).astype(LOW))
            target[:, 4 * half :] = tiny.astype(target.dtype)


def call_attention_backward(rows, scalars, tokens, grad_middle, normed, qkv, probs, attended, joined, first, sums_in, images):
    length, _, width = tokens.shape
    total = normed.shape[1]
    columns = first.shape[2]
    small_at = columns // SMALL - 1

    def of_image(array):
        return pl.BlockSpec((1,) + array.shape[1:], lambda i, s: (i,) + (0,) * (array.ndim - 1))

    def whole(array):
        return pl.BlockSpec(array.shape, lambda i, s: (0,) * array.ndim, pipeline_mode=pl.Buffered(1))

    return pl.pallas_call(
        functools.partial(attention_backward, rows),
        grid_spec=pltpu.PrefetchScalarGridSpec(
            num_scalar_prefetch=1,
            grid=(images,),
            in_specs=[
                pl.BlockSpec((length, images, width), lambda i, s: (0, s[0], 0), pipeline_mode=pl.Buffered(1)),
                whole(grad_middle), of_image(normed), of_image(qkv), of_image(probs), of_image(attended),
                whole(joined),
                pl.BlockSpec((2, width, SMALL), lambda i, s: (0, 0, small_at), pipeline_mode=pl.Buffered(1)),
                whole(sums_in),
            ],
            out_specs=[
                pl.BlockSpec((length, images, width), lambda i, s: (0, 0, 0)),
                pl.BlockSpec((width, columns), lambda i, s: (0, 0)),
                pl.BlockSpec((width, columns), lambda i, s: (0, 0)),
            ],
            scratch_shapes=[
                pltpu.VMEM((total, width), WIDE),
                pltpu.VMEM((total, 3 * width), LOW),
                pltpu.VMEM((width, 3 * width), WIDE),
                pltpu.VMEM((width, width), WIDE),
                pltpu.VMEM((8, 3 * width), WIDE),
                pltpu.VMEM((8, width), WIDE),
                pltpu.VMEM((width // SMALL, length * images, SMALL), WIDE),
                pltpu.VMEM((width // SMALL, length * images, SMALL), WIDE),
            ],
        ),
        out_shape=[
            jax.ShapeDtypeStruct((length, images, width), LOW),
            jax.ShapeDtypeStruct((width, columns), WIDE),
            jax.ShapeDtypeStruct((width, columns), LOW),
        ],
        compiler_params=pltpu.CompilerParams(vmem_limit_bytes=VMEM_LIMIT),
        name="attention_backward",
    )(scalars, tokens, grad_middle, normed, qkv, probs, attended, joined, first, sums_in)


def stages_of(count):
    found = []
    stride = 1
    while stride < count:
        radix = 4 if (count // stride) % 4 == 0 else 2
        found.append((stride, radix))
        stride *= radix
    return found[::-1]


def hop(array, count, offset):
    return lax.ppermute(array, "shard", [(i, i ^ offset) for i in range(count)])


def swap(array):
    return lax.ppermute(array, "tensor", [(0, 1), (1, 0)])


def gather_pieces(piece, count):
    held, owners = piece[None], [0]
    levels = stages_of(count)
    for at, (stride, radix) in enumerate(levels):
        got = [held] + [hop(held, count, k * stride) for k in range(1, radix)]
        marks = [[o ^ (k * stride) for o in owners] for k in range(radix)]
        if at + 1 < len(levels):
            held, owners = jnp.concatenate(got), sum(marks, [])
    return got, marks


def assemble(scalars, got, marks, count):
    arrays = got + [swap(g) for g in got]
    radix = len(got)
    blocks, rows, columns = got[0].shape

    def high_mark(i):
        found = jnp.int32(0)
        for b, mark in enumerate(marks[0]):
            found = jnp.where(i == b, jnp.int32(mark), found)
        return found

    def kernel(scalars, *refs):
        out = refs[-1]
        for half in range(2):
            for a in range(radix):
                place = lax.bitwise_xor(lax.rem(scalars[2], radix), a)
                out[half, pl.ds(place, 1)] = refs[half * radix + a][...]

    return pl.pallas_call(
        kernel,
        grid_spec=pltpu.PrefetchScalarGridSpec(
            num_scalar_prefetch=1,
            grid=(blocks,),
            in_specs=[pl.BlockSpec((1, rows, columns), lambda i, s: (i, 0, 0))] * len(arrays),
            out_specs=pl.BlockSpec(
                (2, radix, rows, columns), lambda i, s: (0, lax.div(lax.bitwise_xor(s[2], high_mark(i)), radix), 0, 0)
            ),
        ),
        out_shape=jax.ShapeDtypeStruct((2, count, rows, columns), LOW),
        compiler_params=pltpu.CompilerParams(vmem_limit_bytes=SMALL_LIMIT),
        name="assemble",
    )(scalars, *arrays)


def combine(scalars, arrays, stride, radix):
    blocks, rows, columns = arrays[0].shape
    high = blocks // radix
    views = [a.reshape(high, radix, rows, columns) for a in arrays]

    def kernel(scalars, *refs):
        outs = refs[len(views) :]
        digit = lax.rem(lax.div(scalars[2], stride), radix)
        for k in range(radix):
            for i in range(outs[0].shape[0]):
                total = None
                for ref in refs[: len(views)]:
                    value = ref[i, lax.bitwise_xor(digit, k)].astype(WIDE)
                    total = value if total is None else total + value
                outs[k][i] = total.astype(outs[k].dtype)

    step = max(1, high // 2)
    return pl.pallas_call(
        kernel,
        grid_spec=pltpu.PrefetchScalarGridSpec(
            num_scalar_prefetch=1,
            grid=(high // step,),
            in_specs=[pl.BlockSpec((step, radix, rows, columns), lambda i, s: (i, 0, 0, 0))] * len(views),
            out_specs=[pl.BlockSpec((step, rows, columns), lambda i, s: (i, 0, 0))] * radix,
        ),
        out_shape=[jax.ShapeDtypeStruct((high, rows, columns), LOW if k else WIDE) for k in range(radix)],
        compiler_params=pltpu.CompilerParams(vmem_limit_bytes=SMALL_LIMIT),
        name="combine",
    )(scalars, *views)


def scatter_rows(scalars, arrays, count, levels, after=None):
    for at, (stride, radix) in enumerate(levels):
        sums = combine(scalars, arrays, stride, radix)
        if at == 0 and after is not None:
            *sums, after = lax.optimization_barrier((*sums, after))
        arrays = [sums[0]] + [hop(sums[k], count, k * stride) for k in range(1, radix)]
    return (arrays, after) if after is not None else arrays


def total_of(refs):
    total = refs[0][0]
    for ref in refs[1:]:
        total = total + ref[0].astype(WIDE)
    return total


def finish_second(arrays, units):
    rows = arrays[0].shape[1]

    def kernel(*refs):
        total = total_of(refs[:-2])
        refs[-2][...] = total[:, :units]
        refs[-1][...] = total[:, units:]

    return pl.pallas_call(
        kernel, out_shape=[jax.ShapeDtypeStruct((rows, units), WIDE)] * 2,
        compiler_params=pltpu.CompilerParams(vmem_limit_bytes=SMALL_LIMIT), name="finish_second"
    )(*arrays)


def finish_first(arrays, half, units):
    rows = arrays[0].shape[1]
    per = units // (2 * half // rows)

    def kernel(*refs):
        outs = refs[len(arrays) :]
        total = total_of(refs[: len(arrays)])
        for i in range(3):
            outs[0][i] = total[:, i * half : (i + 1) * half]
        outs[1][...] = total[:, 3 * half : 4 * half]
        tiny = total[:, 4 * half :]

        def line(at, start, size, columns, shift):
            row = lax.broadcasted_iota(jnp.int32, (rows, columns), 0) - start
            lane = lax.broadcasted_iota(jnp.int32, (rows, columns), 1) - shift
            hit = (row == lane) & (row >= 0) & (row < size)
            return jnp.sum(jnp.where(hit, tiny[:, at : at + 1], 0.0), 0, keepdims=True)

        for i in range(6):
            outs[2 + i][...] = line(i, 0, rows, rows, 0)
        for i in range(2):
            outs[8][i] = line(6, i * (rows // 2), rows // 2, rows // 2, 0)
        wide = line(7, 0, rows, per, 0)
        for c in range(1, per // rows):
            wide = wide + line(7 + c, 0, rows, per, c * rows)
        outs[9][...] = wide

    shapes = [(3, rows, half), (rows, half)] + [(1, rows)] * 6 + [(2, 1, rows // 2), (1, per)]
    return pl.pallas_call(
        kernel, out_shape=[jax.ShapeDtypeStruct(s, WIDE) for s in shapes],
        compiler_params=pltpu.CompilerParams(vmem_limit_bytes=SMALL_LIMIT), name="finish_first"
    )(*arrays)


def join(scalars, array, chunk=50):
    length, images, width = array.shape
    other = swap(array)

    def kernel(scalars, own, other, out):
        out[:, pl.ds(scalars[0], 1)] = own[...][:, None]
        out[:, pl.ds(1 - scalars[0], 1)] = other[...][:, None]

    part = pl.BlockSpec((chunk, images, width), lambda i, s: (i, 0, 0))
    out = pl.pallas_call(
        kernel,
        grid_spec=pltpu.PrefetchScalarGridSpec(
            num_scalar_prefetch=1,
            grid=(pl.cdiv(length, chunk),),
            in_specs=[part, part],
            out_specs=pl.BlockSpec((chunk, 2, images, width), lambda i, s: (i, 0, 0, 0)),
        ),
        out_shape=jax.ShapeDtypeStruct((length, 2, images, width), array.dtype),
        compiler_params=pltpu.CompilerParams(vmem_limit_bytes=SMALL_LIMIT),
        name="join",
    )(scalars, array, other)
    return out.reshape(length, 2 * images, width).transpose(1, 0, 2)


def pack(input_weight, output_t, expand, reduce_t, flat):
    rows, half = output_t.shape
    units = expand.shape[1]
    vectors = flat.shape[0]

    def kernel(w_in, w_out, w_expand, w_reduce, flat, first, second):
        for i in range(3):
            first[:, i * half : (i + 1) * half] = w_in[i]
        first[:, 3 * half : 4 * half] = w_out[...]
        row = lax.broadcasted_iota(jnp.int32, (rows, rows), 0)
        lane = lax.broadcasted_iota(jnp.int32, (rows, rows), 1)
        place = lax.broadcasted_iota(jnp.int32, (rows, SMALL), 1)
        tiny = jnp.zeros((rows, SMALL), WIDE)
        for j in range(vectors):
            column = jnp.sum(jnp.where(row == lane, flat[j : j + 1], 0.0), 1, keepdims=True)
            tiny = jnp.where(place == j, column, tiny)
        first[:, 4 * half :] = tiny.astype(LOW)
        second[:, :units] = w_expand[...]
        second[:, units:] = w_reduce[...]

    return pl.pallas_call(
        kernel,
        out_shape=[
            jax.ShapeDtypeStruct((rows, 4 * half + SMALL), LOW),
            jax.ShapeDtypeStruct((rows, 2 * units), LOW),
        ],
        compiler_params=pltpu.CompilerParams(vmem_limit_bytes=SMALL_LIMIT),
        name="pack",
    )(input_weight, output_t, expand, reduce_t, flat)


def body(shards, tokens, image_counts, input_weight, query_value_bias, output_weight, output_bias, first_gain,
         first_shift, second_gain, second_shift, expand_weight, expand_bias, reduce_weight, reduce_bias, cotangent):
    rows, half = input_weight.shape[1:]
    units = expand_weight.shape[1]
    width = rows * shards
    images = tokens.shape[0] // 2
    scalars = jnp.stack([lax.axis_index("tensor"), image_counts[0], lax.axis_index("shard")]).astype(jnp.int32)
    flat = jnp.concatenate(
        [first_gain, first_shift, second_gain, second_shift, output_bias, reduce_bias, query_value_bias.reshape(-1),
         expand_bias.reshape(-1)]).astype(WIDE).reshape(-1, rows)
    first, second = pack(input_weight, output_weight.T, expand_weight, reduce_weight.T, flat)
    first = assemble(scalars, *gather_pieces(first, shards), shards).reshape(2, width, -1)
    second = assemble(scalars, *gather_pieces(second, shards), shards).reshape(2, width, -1)
    tokens = tokens.transpose(1, 0, 2)
    cotangent = cotangent.transpose(1, 0, 2)
    normed, qkv, probs, attended, middle, joined = call_attention_forward(rows, scalars, tokens, first, images)
    mixed, grad_middle, own, other, sums = call_feed_forward(rows, scalars, middle, cotangent, first, second, images)

    levels = stages_of(shards)[::-1]

    def paired(own, other):
        shape = (shards, rows, -1)
        return [own.reshape(shape), swap(other).reshape(shape)]

    arrays, grad_middle = scatter_rows(scalars, paired(own, other), shards, levels, grad_middle)
    grad_expand, grad_reduce = finish_second(arrays, units)
    token_grad, own, other = call_attention_backward(
        rows, scalars, tokens, grad_middle, normed, qkv, probs, attended, joined, first, sums, images)
    outs = finish_first(scatter_rows(scalars, paired(own, other), shards, levels), half, units)
    gains = [o.reshape(rows) for o in outs[2:8]]
    return (
        join(scalars, mixed),
        join(scalars, token_grad),
        outs[0],
        outs[8],
        outs[1].T,
        gains[4],
        gains[0],
        gains[1],
        gains[2],
        gains[3],
        grad_expand,
        outs[9],
        grad_reduce.T,
        gains[5],
    )


def solution(mesh):
    in_specs = (
        P("shard", None, None),
        P("shard"),
        P(None, "shard", "tensor"),
        P(None, "tensor", "shard"),
        P("tensor", "shard"),
        P("shard"),
        P("shard"),
        P("shard"),
        P("shard"),
        P("shard"),
        P("shard", "tensor"),
        P("tensor", "shard"),
        P("tensor", "shard"),
        P("shard"),
        P("shard", None, None),
    )
    out_specs = in_specs[:1] + in_specs[-1:] + in_specs[2:-1]
    assert mesh.shape["tensor"] == 2
    return jax.shard_map(
        functools.partial(body, mesh.shape["shard"]), mesh=mesh, in_specs=in_specs, out_specs=out_specs, check_vma=False
    )
```
